32 devices in a mesh: grp: 2 (over x), con: 16 (over z, y, core).
Axes of the slice: x: 2, y: 2, z: 4, core: 2. Of those that a mesh axis runs over, the one named last changes fastest.
Arguments:
- matrix: float32 [32768, 2048], P(('grp', 'con')), parts along dimension 0, may hold values from -0.046875 to 0.046875
- bounds_rhs: float32 [32768, 128], P(('grp', 'con')), parts along dimension 0, may hold values from -3 to 3
- costs: float32 [4096, 128], P(('grp', 'con')), parts along dimension 0, may hold values from -12 to 12
- upper: float32 [4096], P(('grp', 'con')), parts along dimension 0, may hold values from 0.5 to 2
- bound_mask: int32 [4096], P(('grp', 'con')), parts along dimension 0, may hold values 0 or 1
- node_map: int32 [3, 256], P(None, 'grp'), parts along dimension 1, may hold values from 0 to 63, as said below
- weights: int32 [256], P('grp'), parts along dimension 0, may hold values from 1 to 10
Outputs:
- primal: float32 [4096, 128], P(('grp', 'con')), parts along dimension 0
- dual: float32 [32768, 128], P(('grp', 'con')), parts along dimension 0
- multipliers: float32 [4096, 128], P(('grp', 'con')), parts along dimension 0
- gaps: float32 [4], P('grp'), parts along dimension 0
The draws below stay inside these ranges and needn't reach their ends.
There are 2 independent parts, one for each index of `grp`. The reference program is written for one: setup_inputs(seed, part) draws one part's arguments, and reference() takes and returns one part's arrays. A program takes and returns all parts, laid end to end along the dimension named above; each array names one. Nothing has to cross between parts.
Inputs may be any that keep to these rules, and one draw needn't show every extreme that they name: `node_map`: row t numbers the 4 ** (t + 1) nodes of that section; each node holds 128 / 4 ** (t + 1) scenarios, and the nodes of row t + 1 split those of row t.
All inputs are finite; a program needn't handle non-finite values. No bound on the sum of `bound_mask` on one device may be relied on, other than what follows from the above.
Results may differ from the reference program's by a relative error of at most 0.0001.
Values sent between devices are 32-bit elements; how exact they have to be, the bound alone decides.
A program may use at most 64 MiB of HBM per device.

```python
import math
import jax
import jax.numpy as jnp
from jax import lax

N = 2048
SCEN = 128
LEVELS = 3
OUTER = 2
INNER = 2
M = 16384


def draw_costs(key, part):
    column = jnp.arange(N, dtype=jnp.float32)[:, None] / N
    base = jnp.clip(jax.random.normal(key, (N, SCEN), jnp.float32), -4.0, 4.0)
    return base * 0.3 * 10.0 ** column


def draw_node_map(key, part):
    ordering = jax.random.permutation(jax.random.fold_in(key, 7), SCEN).astype(jnp.int32)
    stacked = [ordering // (SCEN // 4 ** (depth_level + 1)) for depth_level in range(LEVELS)]
    return jnp.stack(stacked).astype(jnp.int32)


def set_ends(result, own_key, low, largest):
    spot = [jax.random.randint(jax.random.fold_in(own_key, axis), (), 0, length) for axis, length in enumerate(result.shape)]
    widest = result.shape.index(max(result.shape))
    beside = spot[:widest] + [(spot[widest] + 1) % result.shape[widest]] + spot[widest + 1:]
    return result.at[tuple(spot)].set(low).at[tuple(beside)].set(largest)


def block_scale(stream_key, dims, cuts, least, top_value):
    def one(position, shards_of):
        heights = jax.random.uniform(jax.random.fold_in(jax.random.fold_in(stream_key, 6), position), (shards_of,), jnp.float32, least / len(cuts), top_value / len(cuts))
        return jnp.repeat(jnp.exp(heights), dims[position] // shards_of).reshape((-1,) + (1,) * (len(dims) - position - 1))

    gain = one(*cuts[0])
    for cut in cuts[1:]:
        gain = gain * one(*cut)
    return gain


def centred(rng, shape, scale, most, pieces=(), kind=jnp.bfloat16):
    gain = block_scale(rng, shape, pieces, -0.22, 0.18) if pieces else 1.0
    result = jax.random.normal(rng, shape, jnp.float32) * scale * gain
    return jnp.minimum(jnp.maximum(result, -most), most).astype(kind)


def setup_inputs(seed: int = 0, part: int = 0) -> dict:
    arg_keys = jax.random.split(jax.random.key(seed), 8)
    own_keys = jax.random.split(jax.random.fold_in(arg_keys[7], part), 8)
    return {
        "matrix": centred(own_keys[0], (M, N), M ** -0.5, 0.046875, ((0, 16),), jnp.float32),
        "bounds_rhs": centred(own_keys[1], (M, SCEN), 0.5, 3.0, ((0, 16),), jnp.float32),
        "costs": draw_costs(jax.random.fold_in(jax.random.fold_in(arg_keys[7], part), 71), part),
        "upper": jnp.clip(jnp.exp(math.log(2.0) - 1.3862944 * jax.random.uniform(own_keys[3], (N,), jnp.float32) ** block_scale(own_keys[3], (N,), ((0, 16),), -0.2, 0.2)), 0.5, 2.0),
        "bound_mask": set_ends((jax.random.randint(own_keys[4], (N,), 0, 2) < 1).astype(jnp.int32), jax.random.fold_in(own_keys[4], 1), 0, 1),
        "node_map": draw_node_map(jax.random.fold_in(jax.random.fold_in(arg_keys[7], part), 71), part),
        "weights": set_ends(jax.random.randint(own_keys[6], (SCEN,), 1, 11), jax.random.fold_in(own_keys[6], 1), 1, 10).astype(jnp.int32),
    }


highest = lax.Precision.HIGHEST
step_primal = 0.4
step_dual = 0.6
penalty = 1.0


def node_average(node_map, weights):
    weight_float = weights.astype(jnp.float32)
    probability = weight_float / jnp.sum(weight_float)
    same_node = (node_map[:, :, None] == node_map[:, None, :]).astype(jnp.float32)
    node_mass = same_node * probability[None, None, :]
    return node_mass / jnp.sum(node_mass, axis=2, keepdims=True), probability


def consensus(primal, averaging, column_index):
    averaged = jnp.einsum("tsr,jr->tjs", averaging, primal, precision=highest)
    section_of = column_index % (averaging.shape[0] + 1)
    section_hot = (section_of[None, :] == jnp.arange(averaging.shape[0], dtype=jnp.int32)[:, None]).astype(jnp.float32)
    free_cols = 1.0 - jnp.sum(section_hot, axis=0)
    return jnp.sum(section_hot[:, :, None] * averaged, axis=0) + free_cols[:, None] * primal


def primal_step(primal, costs, multipliers, average, transposed, upper, flags, prox_weight):
    gradient = costs + multipliers + prox_weight * (primal - average) + transposed
    moved = jnp.maximum(primal - step_primal * gradient, 0.0)
    return jnp.where(flags[:, None] > 0, jnp.minimum(moved, upper[:, None]), moved)


def reference(matrix, bounds_rhs, costs, upper, bound_mask, node_map, weights):
    averaging, probability = node_average(node_map, weights)
    column_index = jnp.arange(N, dtype=jnp.int32)
    flags = bound_mask.astype(jnp.float32)
    primal = jnp.zeros((N, SCEN), jnp.float32)
    multipliers = jnp.zeros((N, SCEN), jnp.float32)
    average = jnp.zeros((N, SCEN), jnp.float32)
    transposed = jnp.zeros((N, SCEN), jnp.float32)
    dual = jnp.zeros((M, SCEN), jnp.float32)
    partials = []
    for outer_turn in range(OUTER):
        prox_weight = 0.0 if outer_turn == 0 else penalty
        for inner_turn in range(INNER):
            moved = primal_step(primal, costs, multipliers, average, transposed, upper, flags, prox_weight)
            extrap = 2.0 * moved - primal
            product = jnp.dot(matrix, extrap, precision=highest)
            dual = jnp.maximum(dual + step_dual * (product - bounds_rhs), 0.0)
            primal = moved
            if outer_turn < OUTER - 1 or inner_turn < INNER - 1:
                transposed = lax.dot_general(matrix, dual, (((0,), (0,)), ((), ())), precision=highest)
        average = consensus(primal, averaging, column_index)
        deviation = primal - average
        multipliers = multipliers + penalty * deviation
        partials.append(jnp.sum(deviation * deviation * probability[None, :]) / N)
    return primal, dual, multipliers, jnp.stack(partials)
```

```python
import jax
import jax.numpy as jnp
from jax import lax
from jax.sharding import PartitionSpec as P

N = 2048
OUTER = 2
INNER = 2


highest = lax.Precision.HIGHEST
step_primal = 0.4
step_dual = 0.6
penalty = 1.0


def node_average(node_map, weights):
    weight_float = weights.astype(jnp.float32)
    probability = weight_float / jnp.sum(weight_float)
    same_node = (node_map[:, :, None] == node_map[:, None, :]).astype(jnp.float32)
    node_mass = same_node * probability[None, None, :]
    return (node_mass / jnp.sum(node_mass, axis=2, keepdims=True), probability)


def consensus(primal, averaging, column_index):
    averaged = jnp.einsum("tsr,jr->tjs", averaging, primal, precision=highest)
    section_of = column_index % (averaging.shape[0] + 1)
    section_hot = (
        section_of[None, :] == jnp.arange(averaging.shape[0], dtype=jnp.int32)[:, None]
    ).astype(jnp.float32)
    free_cols = 1.0 - jnp.sum(section_hot, axis=0)
    return jnp.sum(section_hot[:, :, None] * averaged, axis=0) + free_cols[:, None] * primal


def primal_step(primal, costs, multipliers, average, transposed, upper, flags, prox_weight):
    gradient = costs + multipliers + prox_weight * (primal - average) + transposed
    moved = jnp.maximum(primal - step_primal * gradient, 0.0)
    return jnp.where(flags[:, None] > 0, jnp.minimum(moved, upper[:, None]), moved)


def apply_rows(matrix, extrap):
    return jnp.dot(matrix, lax.all_gather(extrap, "con", axis=0, tiled=True), precision=lax.Precision.HIGH)


def apply_columns(matrix, dual):
    return lax.psum_scatter(
        lax.dot_general(matrix, dual, (((0,), (0,)), ((), ())), precision=lax.Precision.HIGH),
        "con",
        scatter_dimension=0,
        tiled=True,
    )


def body(matrix, bounds_rhs, costs, upper, bound_mask, node_map, weights):
    own_cols = costs.shape[0]
    scenario_count = costs.shape[1]
    averaging, probability = node_average(node_map, weights)
    start_col = lax.axis_index("con") * own_cols
    costs_all, upper_all, flags_all = (costs, upper, bound_mask.astype(jnp.float32))
    width = costs_all.shape[0]
    column_index = start_col + jnp.arange(width, dtype=jnp.int32)
    primal = jnp.zeros((width, scenario_count), jnp.float32)
    multipliers = jnp.zeros((width, scenario_count), jnp.float32)
    average = jnp.zeros((width, scenario_count), jnp.float32)
    transposed = jnp.zeros((width, scenario_count), jnp.float32)
    dual = jnp.zeros(bounds_rhs.shape, jnp.float32)
    partials = []
    for outer_turn in range(OUTER):
        prox_weight = 0.0 if outer_turn == 0 else penalty
        for inner_turn in range(INNER):
            moved = primal_step(
                primal,
                costs_all,
                multipliers,
                average,
                transposed,
                upper_all,
                flags_all,
                prox_weight,
            )
            extrap = 2.0 * moved - primal
            product = apply_rows(matrix, extrap)
            dual = jnp.maximum(dual + step_dual * (product - bounds_rhs), 0.0)
            primal = moved
            if outer_turn < OUTER - 1 or inner_turn < INNER - 1:
                transposed = apply_columns(matrix, dual)
        average = consensus(primal, averaging, column_index)
        deviation = primal - average
        multipliers = multipliers + penalty * deviation
        partial_value = jnp.sum(deviation * deviation * probability[None, :]) / N
        partial_value = lax.psum(partial_value, "con")
        partials.append(partial_value)
    gaps = jnp.stack(partials)
    return (primal, dual, multipliers, gaps)


def solution(mesh):
    placed = (
        P(("grp", "con"), None),
        P(("grp", "con"), None),
        P(("grp", "con"), None),
        P(("grp", "con")),
        P(("grp", "con")),
        P(None, "grp"),
        P("grp"),
    )
    return jax.shard_map(
        body,
        mesh=mesh,
        in_specs=placed,
        out_specs=(
            P(("grp", "con"), None),
            P(("grp", "con"), None),
            P(("grp", "con"), None),
            P("grp"),
        ),
        check_vma=False,
    )
```

```python
import functools

import jax
import jax.numpy as jnp
from jax import lax
from jax.experimental import pallas as pl
from jax.experimental.pallas import tpu as pltpu
from jax.sharding import PartitionSpec as P

OUTER = 2
INNER = 2
step_primal = 0.4
step_dual = 0.6
penalty = 1.0
MESH = pl.DeviceIdType.MESH
f32 = jnp.float32
bf16 = jnp.bfloat16


def split(value):
    high = value.astype(bf16)
    return high, (value - high.astype(f32)).astype(bf16)


def halves(wide):
    return wide[:, : wide.shape[1] // 2] + wide[:, wide.shape[1] // 2 :]


def kernel(
    n, total_cols,
    matrix, rhs, costs, upper, mask, node_map, weights,
    primal, dual, multipliers, gaps,
    staged, rows_cat, cols_cat, gathered, product, dual_cat, part, core_in, row_in, far_in,
    average, transposed, cap, averaging, gap_part, gap_all,
    load_sem, agz_s, agz_r, agy_s, agy_r, agc_s, agc_r, rsc_s, rsc_r, rsy_s, rsy_r, rsz_s, rsz_r, gap_s, gap_r,
):
    me = lax.axis_index("con")
    zs = n // 4
    z, y, c = me // 4, lax.rem(me // 2, 2), lax.rem(me, 2)
    width, scen = costs.shape
    rows = rhs.shape[0]
    chunk = 4 * width
    tile = 128

    def place(pz, py, pc):
        return pz * 4 + py * 2 + pc

    other_core, other_row = place(z, y, 1 - c), place(z, 1 - y, c)

    def remote(src, dst, send, recv, target):
        return pltpu.make_async_remote_copy(
            src_ref=src, dst_ref=dst, send_sem=send, recv_sem=recv,
            device_id={"con": target}, device_id_type=MESH,
        )

    def load(dz):
        at = lax.rem(z - dz + zs, zs)
        return pltpu.make_async_copy(
            matrix.at[:, pl.ds(pl.multiple_of(at * chunk, chunk), chunk)], staged.at[at], load_sem.at[dz]
        )

    for dz in range(zs):
        load(dz).start()

    barrier = pltpu.get_barrier_semaphore()
    for step in range(1, n):
        pl.semaphore_signal(barrier, inc=1, device_id={"con": lax.rem(me + step, n)}, device_id_type=MESH)

    bound = jnp.where(mask[...] > 0, upper[...], jnp.inf)
    cap[...] = jnp.transpose(jnp.broadcast_to(bound, (scen, width)))
    for ref in (primal, multipliers, average, transposed, dual, gap_part):
        ref[...] = jnp.zeros_like(ref)
    weight = weights[...].astype(f32)
    probability = weight / jnp.sum(weight)
    pl.semaphore_wait(barrier, n - 1)

    def prepare():
        by_row = jnp.transpose(jnp.broadcast_to(probability, (scen, scen)))
        for level in range(node_map.shape[0]):
            nodes = jnp.broadcast_to(node_map[pl.ds(level, 1), :].astype(f32), (scen, scen))
            mass = jnp.where(nodes == jnp.transpose(nodes), by_row, 0.0)
            averaging[level] = mass / jnp.sum(mass, axis=0, keepdims=True)

    def convert(dz):
        at = lax.rem(z - dz + zs, zs)
        load(dz).wait()

        @pl.loop(0, rows // tile)
        def _(step):
            here = pl.ds(pl.multiple_of(step * tile, tile), tile)
            block = staged[at, here, :]
            high, low = split(block)
            rows_cat[at, here, :chunk] = high
            rows_cat[at, here, chunk:] = low
            high, low = split(jnp.transpose(block))
            cols_cat[at, :, here] = high
            cols_cat[at, :, pl.ds(pl.multiple_of(rows + step * tile, tile), tile)] = low

    def agree(turn):
        now = primal[...]
        section = lax.rem(me * width + lax.broadcasted_iota(jnp.int32, now.shape, 0), averaging.shape[0] + 1)
        mean = now
        for level in range(averaging.shape[0]):
            at_level = jnp.dot(now, averaging[level], precision=lax.Precision.HIGHEST, preferred_element_type=f32)
            mean = jnp.where(section == level, at_level, mean)
        average[...] = mean
        deviation = now - mean
        multipliers[...] = multipliers[...] + penalty * deviation
        gap_part[pl.ds(turn, 1), :] = jnp.sum(deviation * deviation * probability, axis=0, keepdims=True)

    def gap_copy(step):
        return remote(gap_all.at[me], gap_all.at[me], gap_s.at[step], gap_r.at[step], lax.rem(me + step, n))

    last = OUTER * INNER - 1

    def one_pass(turn, carry):
        before = primal[...]
        prox = jnp.where(turn >= INNER, penalty, 0.0).astype(f32)
        gradient = costs[...] + multipliers[...] + prox * (before - average[...]) + transposed[...]
        moved = jnp.minimum(jnp.maximum(before - step_primal * gradient, 0.0), cap[...])
        primal[...] = moved
        gathered[me] = 2.0 * moved - before

        def slot_copy(slot, send, recv, target):
            copy = remote(gathered.at[slot], gathered.at[slot], send, recv, target)
            copy.start()
            return copy

        far, near, core = {}, {}, {}
        core[0, 0] = slot_copy(me, agc_s.at[0], agc_r.at[0], other_core)
        near[0] = slot_copy(me, agy_s.at[0], agy_r.at[0], other_row)
        for dz in range(1, zs):
            far[dz] = slot_copy(me, agz_s.at[dz], agz_r.at[dz], place(lax.rem(z + dz, zs), y, c))

        @pl.when(turn == 0)
        def _():
            prepare()

        @pl.when(lax.rem(turn, INNER) == INNER - 1)
        def _():
            agree(turn // INNER)

        @pl.when(turn == last)
        def _():
            gap_all[me] = gap_part[...]
            for step in range(1, n):
                gap_copy(step).start()

        def from_far(dz):
            if dz > 0:
                far[dz].wait_recv()
                slot = place(lax.rem(z - dz + zs, zs), y, c)
                near[dz] = slot_copy(slot, agy_s.at[dz], agy_r.at[dz], other_row)
                core[dz, 0] = slot_copy(slot, agc_s.at[2 * dz], agc_r.at[2 * dz], other_core)

        def from_near(dz):
            near[dz].wait_recv()
            slot = place(lax.rem(z - dz + zs, zs), 1 - y, c)
            core[dz, 1] = slot_copy(slot, agc_s.at[2 * dz + 1], agc_r.at[2 * dz + 1], other_core)

        def multiply(dz):
            at = lax.rem(z - dz + zs, zs)

            @pl.when(turn == 0)
            def _():
                convert(dz)

            core[dz, 0].wait_recv()
            core[dz, 1].wait_recv()
            arrived = gathered[pl.ds(at * 4, 4)].reshape(chunk, scen)
            wide = jnp.concatenate(split(arrived), axis=1)
            wide = jnp.concatenate([wide, wide], axis=0)
            term = halves(jnp.dot(rows_cat[at], wide, preferred_element_type=f32))
            if dz == 0:
                product[...] = term
            else:
                product[...] += term

        for dz in range(zs + 2):
            if dz < zs:
                from_far(dz)
            if 1 <= dz <= zs:
                from_near(dz - 1)
            if dz >= 2:
                multiply(dz - 2)
        for copy in [*far.values(), *near.values(), *core.values()]:
            copy.wait_send()

        now = jnp.maximum(dual[...] + step_dual * (product[...] - rhs[...]), 0.0)
        dual[...] = now

        @pl.when(turn < last)
        def _():
            wide = jnp.concatenate(split(now), axis=1)
            dual_cat[:rows] = wide
            dual_cat[rows:] = wide
            to_core, to_row, to_far = {}, {}, {}

            def transpose(dz):
                at = lax.rem(z + dz, zs)
                term = halves(jnp.dot(cols_cat[at], dual_cat[...], preferred_element_type=f32))
                part[pl.ds(at * 4, 4)] = term.reshape(4, width, scen)
                for k, py in enumerate((1 - y, y)):
                    index = 2 * dz + k
                    to_core[dz, k] = remote(
                        part.at[place(at, py, 1 - c)], core_in.at[index], rsc_s.at[index], rsc_r.at[index], other_core
                    )
                    to_core[dz, k].start()

            def add_core(dz):
                at = lax.rem(z + dz, zs)
                for k, py in enumerate((1 - y, y)):
                    to_core[dz, k].wait_recv()
                    slot = place(at, py, c)
                    part[slot] = part[slot] + core_in[2 * dz + k]
                    if k == 0:
                        to_row[dz] = remote(part.at[slot], row_in.at[dz], rsy_s.at[dz], rsy_r.at[dz], other_row)
                        to_row[dz].start()

            def add_row(dz):
                at = lax.rem(z + dz, zs)
                slot = place(at, y, c)
                to_row[dz].wait_recv()
                part[slot] = part[slot] + row_in[dz]
                if dz > 0:
                    to_far[dz] = remote(part.at[slot], far_in.at[dz], rsz_s.at[dz], rsz_r.at[dz], place(at, y, c))
                    to_far[dz].start()

            order = [*range(1, zs), 0]
            for step in range(zs + 2):
                if step < zs:
                    transpose(order[step])
                if 2 <= step:
                    add_row_at = step - 2
                else:
                    add_row_at = None
                if 1 <= step <= zs:
                    add_core(order[step - 1])
                if add_row_at is not None:
                    add_row(order[add_row_at])
            total = part[me]
            for dz in range(1, zs):
                to_far[dz].wait_recv()
                total = total + far_in[dz]
            transposed[...] = total
            for copy in [*to_core.values(), *to_row.values(), *to_far.values()]:
                copy.wait_send()

        return carry

    lax.fori_loop(0, last + 1, one_pass, 0)
    for step in range(1, n):
        gap_copy(step).wait_recv()
    everyone = jnp.sum(gap_all[...], axis=0)
    gaps[...] = jnp.broadcast_to(jnp.sum(everyone, axis=1, keepdims=True) / total_cols, gaps.shape)
    for step in range(1, n):
        gap_copy(step).wait_send()


def body(n, matrix, bounds_rhs, costs, upper, bound_mask, node_map, weights):
    rows, total_cols = matrix.shape
    width, scen = costs.shape
    zs = n // 4
    vmem = pl.BlockSpec(memory_space=pltpu.VMEM)
    dma = pltpu.SemaphoreType.DMA
    primal, dual, multipliers, gaps = pl.pallas_call(
        functools.partial(kernel, n, total_cols),
        out_shape=(
            jax.ShapeDtypeStruct((width, scen), f32),
            jax.ShapeDtypeStruct((rows, scen), f32),
            jax.ShapeDtypeStruct((width, scen), f32),
            jax.ShapeDtypeStruct((8, 128), f32),
        ),
        in_specs=[pl.BlockSpec(memory_space=pl.ANY)] + [vmem] * 6,
        out_specs=(vmem,) * 4,
        scratch_shapes=[
            pltpu.VMEM((zs, rows, 4 * width), f32),
            pltpu.VMEM((zs, rows, 8 * width), bf16),
            pltpu.VMEM((zs, 4 * width, 2 * rows), bf16),
            pltpu.VMEM((n, width, scen), f32),
            pltpu.VMEM((rows, scen), f32),
            pltpu.VMEM((2 * rows, 2 * scen), bf16),
            pltpu.VMEM((n, width, scen), f32),
            pltpu.VMEM((2 * zs, width, scen), f32),
            pltpu.VMEM((zs, width, scen), f32),
            pltpu.VMEM((zs, width, scen), f32),
            pltpu.VMEM((width, scen), f32),
            pltpu.VMEM((width, scen), f32),
            pltpu.VMEM((width, scen), f32),
            pltpu.VMEM((node_map.shape[0], scen, scen), f32),
            pltpu.VMEM((8, scen), f32),
            pltpu.VMEM((n, 8, scen), f32),
            dma((zs,)),
            dma((zs,)), dma((zs,)), dma((zs,)), dma((zs,)), dma((2 * zs,)), dma((2 * zs,)),
            dma((2 * zs,)), dma((2 * zs,)), dma((zs,)), dma((zs,)), dma((zs,)), dma((zs,)),
            dma((n,)), dma((n,)),
        ],
        compiler_params=pltpu.CompilerParams(collective_id=0, has_side_effects=True, vmem_limit_bytes=56 << 20),
    )(matrix, bounds_rhs, costs, upper[None, :], bound_mask[None, :], node_map, weights[None, :])
    return primal, dual, multipliers, gaps[:OUTER, 0]


def solution(mesh):
    placed = (
        P(("grp", "con"), None),
        P(("grp", "con"), None),
        P(("grp", "con"), None),
        P(("grp", "con")),
        P(("grp", "con")),
        P(None, "grp"),
        P("grp"),
    )
    return jax.shard_map(
        functools.partial(body, mesh.shape["con"]),
        mesh=mesh,
        in_specs=placed,
        out_specs=(
            P(("grp", "con"), None),
            P(("grp", "con"), None),
            P(("grp", "con"), None),
            P("grp"),
        ),
        check_vma=False,
    )
```

```python
import functools

import jax
import jax.numpy as jnp
from jax import lax
from jax.experimental import pallas as pl
from jax.experimental.pallas import tpu as pltpu
from jax.sharding import PartitionSpec as P

OUTER = 2
INNER = 2
step_primal = 0.4
step_dual = 0.6
penalty = 1.0
MESH = pl.DeviceIdType.MESH
f32 = jnp.float32
bf16 = jnp.bfloat16


def split(value):
    high = value.astype(bf16)
    return high, (value - high.astype(f32)).astype(bf16)


def halves(wide):
    return wide[:, : wide.shape[1] // 2] + wide[:, wide.shape[1] // 2 :]


def across(z, step):
    bit, partner = 1, z
    while bit <= step:
        if step & bit:
            partner = partner + bit * (1 - 2 * lax.rem(z // bit, 2))
        bit *= 2
    return partner


def kernel(
    n, total_cols,
    matrix, rhs, costs, upper, mask, node_map, weights,
    primal, dual, multipliers, gaps,
    staged, rows_cat, cols_cat, gathered, product, dual_cat, part, core_in, row_in, far_in,
    average, transposed, cap, averaging, gap_part, gap_all,
    load_sem, agz_s, agz_r, agy_s, agy_r, agc_s, agc_r, rsc_s, rsc_r, rsy_s, rsy_r, rsz_s, rsz_r, gap_s, gap_r,
):
    me = lax.axis_index("con")
    zs = n // 4
    z, y, c = me // 4, lax.rem(me // 2, 2), lax.rem(me, 2)
    width, scen = costs.shape
    rows = rhs.shape[0]
    chunk = 4 * width
    tile = 128

    def place(pz, py, pc):
        return pz * 4 + py * 2 + pc

    other_core, other_row = place(z, y, 1 - c), place(z, 1 - y, c)

    def remote(src, dst, send, recv, target):
        return pltpu.make_async_remote_copy(
            src_ref=src, dst_ref=dst, send_sem=send, recv_sem=recv,
            device_id={"con": target}, device_id_type=MESH,
        )

    def load(dz):
        at = across(z, dz)
        return pltpu.make_async_copy(
            matrix.at[:, pl.ds(pl.multiple_of(at * chunk, chunk), chunk)], staged.at[at], load_sem.at[dz]
        )

    for dz in range(zs):
        load(dz).start()

    barrier = pltpu.get_barrier_semaphore()
    for step in range(1, n):
        pl.semaphore_signal(barrier, inc=1, device_id={"con": lax.rem(me + step, n)}, device_id_type=MESH)

    bound = jnp.where(mask[...] > 0, upper[...], jnp.inf)
    cap[...] = jnp.transpose(jnp.broadcast_to(bound, (scen, width)))
    for ref in (primal, multipliers, average, transposed, dual, gap_part):
        ref[...] = jnp.zeros_like(ref)
    weight = weights[...].astype(f32)
    probability = weight / jnp.sum(weight)
    pl.semaphore_wait(barrier, n - 1)

    def prepare():
        by_row = jnp.transpose(jnp.broadcast_to(probability, (scen, scen)))
        for level in range(node_map.shape[0]):
            nodes = jnp.broadcast_to(node_map[pl.ds(level, 1), :].astype(f32), (scen, scen))
            mass = jnp.where(nodes == jnp.transpose(nodes), by_row, 0.0)
            averaging[level] = mass / jnp.sum(mass, axis=0, keepdims=True)

    def convert(dz):
        at = across(z, dz)
        load(dz).wait()

        @pl.loop(0, rows // tile)
        def _(step):
            here = pl.ds(pl.multiple_of(step * tile, tile), tile)
            block = staged[at, here, :]
            high, low = split(block)
            rows_cat[at, here, :chunk] = high
            rows_cat[at, here, chunk:] = low
            high, low = split(jnp.transpose(block))
            cols_cat[at, :, here] = high
            cols_cat[at, :, pl.ds(pl.multiple_of(rows + step * tile, tile), tile)] = low

    def agree(turn):
        now = primal[...]
        section = lax.rem(me * width + lax.broadcasted_iota(jnp.int32, now.shape, 0), averaging.shape[0] + 1)
        mean = now
        for level in range(averaging.shape[0]):
            at_level = jnp.dot(now, averaging[level], precision=lax.Precision.HIGHEST, preferred_element_type=f32)
            mean = jnp.where(section == level, at_level, mean)
        average[...] = mean
        deviation = now - mean
        multipliers[...] = multipliers[...] + penalty * deviation
        gap_part[pl.ds(turn, 1), :] = jnp.sum(deviation * deviation * probability, axis=0, keepdims=True)

    def gap_copy(step):
        return remote(gap_all.at[me], gap_all.at[me], gap_s.at[step], gap_r.at[step], lax.rem(me + step, n))

    last = OUTER * INNER - 1

    def one_pass(turn, carry):
        before = primal[...]
        prox = jnp.where(turn >= INNER, penalty, 0.0).astype(f32)
        gradient = costs[...] + multipliers[...] + prox * (before - average[...]) + transposed[...]
        moved = jnp.minimum(jnp.maximum(before - step_primal * gradient, 0.0), cap[...])
        primal[...] = moved
        gathered[me] = 2.0 * moved - before

        def slot_copy(slot, send, recv, target):
            copy = remote(gathered.at[slot], gathered.at[slot], send, recv, target)
            copy.start()
            return copy

        far, near, core = {}, {}, {}
        core[0, 0] = slot_copy(me, agc_s.at[0], agc_r.at[0], other_core)
        near[0] = slot_copy(me, agy_s.at[0], agy_r.at[0], other_row)
        for dz in range(1, zs):
            far[dz] = slot_copy(me, agz_s.at[dz], agz_r.at[dz], place(across(z, dz), y, c))

        @pl.when(turn == 0)
        def _():
            prepare()
            convert(0)

        @pl.when(lax.rem(turn, INNER) == INNER - 1)
        def _():
            agree(turn // INNER)

        @pl.when(turn == last)
        def _():
            gap_all[me] = gap_part[...]
            for step in range(1, n):
                gap_copy(step).start()

        def from_far(dz):
            if dz > 0:
                far[dz].wait_recv()
                slot = place(across(z, dz), y, c)
                near[dz] = slot_copy(slot, agy_s.at[dz], agy_r.at[dz], other_row)
                core[dz, 0] = slot_copy(slot, agc_s.at[2 * dz], agc_r.at[2 * dz], other_core)

        def from_near(dz):
            near[dz].wait_recv()
            slot = place(across(z, dz), 1 - y, c)
            core[dz, 1] = slot_copy(slot, agc_s.at[2 * dz + 1], agc_r.at[2 * dz + 1], other_core)

        def multiply(dz):
            at = across(z, dz)

            if dz + 1 < zs:

                @pl.when(turn == 0)
                def _():
                    convert(dz + 1)

            core[dz, 0].wait_recv()
            core[dz, 1].wait_recv()
            arrived = gathered[pl.ds(at * 4, 4)].reshape(chunk, scen)
            wide = jnp.concatenate(split(arrived), axis=1)
            wide = jnp.concatenate([wide, wide], axis=0)
            term = halves(jnp.dot(rows_cat[at], wide, preferred_element_type=f32))
            if dz == 0:
                product[...] = term
            else:
                product[...] += term

        for dz in range(zs):
            from_far(dz)
        for dz in range(zs):
            from_near(dz)
            if dz >= 1:
                multiply(dz - 1)
        multiply(zs - 1)
        for copy in [*far.values(), *near.values(), *core.values()]:
            copy.wait_send()

        now = jnp.maximum(dual[...] + step_dual * (product[...] - rhs[...]), 0.0)
        dual[...] = now

        @pl.when(turn < last)
        def _():
            wide = jnp.concatenate(split(now), axis=1)
            dual_cat[:rows] = wide
            dual_cat[rows:] = wide
            to_core, to_row, to_far = {}, {}, {}

            def transpose(dz):
                at = across(z, dz)
                term = halves(jnp.dot(cols_cat[at], dual_cat[...], preferred_element_type=f32))
                part[pl.ds(at * 4, 4)] = term.reshape(4, width, scen)
                for k, py in enumerate((1 - y, y)):
                    index = 2 * dz + k
                    to_core[dz, k] = remote(
                        part.at[place(at, py, 1 - c)], core_in.at[index], rsc_s.at[index], rsc_r.at[index], other_core
                    )
                    to_core[dz, k].start()

            def add_core(dz):
                at = across(z, dz)
                for k, py in enumerate((1 - y, y)):
                    to_core[dz, k].wait_recv()
                    slot = place(at, py, c)
                    part[slot] = part[slot] + core_in[2 * dz + k]
                    if k == 0:
                        to_row[dz] = remote(part.at[slot], row_in.at[dz], rsy_s.at[dz], rsy_r.at[dz], other_row)
                        to_row[dz].start()

            def add_row(dz):
                at = across(z, dz)
                slot = place(at, y, c)
                to_row[dz].wait_recv()
                part[slot] = part[slot] + row_in[dz]
                if dz > 0:
                    to_far[dz] = remote(part.at[slot], far_in.at[dz], rsz_s.at[dz], rsz_r.at[dz], place(at, y, c))
                    to_far[dz].start()

            order = [*range(zs - 1, -1, -1)]
            for step in range(zs + 1):
                if step < zs:
                    transpose(order[step])
                if step >= 1:
                    add_core(order[step - 1])
            for dz in order:
                add_row(dz)
            total = part[me]
            for dz in range(1, zs):
                to_far[dz].wait_recv()
                total = total + far_in[dz]
            transposed[...] = total
            for copy in [*to_core.values(), *to_row.values(), *to_far.values()]:
                copy.wait_send()

        return carry

    lax.fori_loop(0, last + 1, one_pass, 0)
    for step in range(1, n):
        gap_copy(step).wait_recv()
    everyone = jnp.sum(gap_all[...], axis=0)
    gaps[...] = jnp.broadcast_to(jnp.sum(everyone, axis=1, keepdims=True) / total_cols, gaps.shape)
    for step in range(1, n):
        gap_copy(step).wait_send()


def finish(primal_in, dual_in, multipliers_in, gaps_in, primal, dual, multipliers, gaps):
    primal[...] = primal_in[...]
    dual[...] = dual_in[...]
    multipliers[...] = multipliers_in[...]
    for turn in range(gaps.shape[0]):
        gaps[turn] = jnp.max(gaps_in[pl.ds(turn, 1), :])


def body(n, matrix, bounds_rhs, costs, upper, bound_mask, node_map, weights):
    rows, total_cols = matrix.shape
    width, scen = costs.shape
    zs = n // 4
    vmem = pl.BlockSpec(memory_space=pltpu.VMEM)
    dma = pltpu.SemaphoreType.DMA
    primal, dual, multipliers, gaps = pl.pallas_call(
        functools.partial(kernel, n, total_cols),
        out_shape=(
            jax.ShapeDtypeStruct((width, scen), f32),
            jax.ShapeDtypeStruct((rows, scen), f32),
            jax.ShapeDtypeStruct((width, scen), f32),
            jax.ShapeDtypeStruct((8, 128), f32),
        ),
        in_specs=[pl.BlockSpec(memory_space=pl.ANY)] + [vmem] * 6,
        out_specs=(vmem,) * 4,
        scratch_shapes=[
            pltpu.VMEM((zs, rows, 4 * width), f32),
            pltpu.VMEM((zs, rows, 8 * width), bf16),
            pltpu.VMEM((zs, 4 * width, 2 * rows), bf16),
            pltpu.VMEM((n, width, scen), f32),
            pltpu.VMEM((rows, scen), f32),
            pltpu.VMEM((2 * rows, 2 * scen), bf16),
            pltpu.VMEM((n, width, scen), f32),
            pltpu.VMEM((2 * zs, width, scen), f32),
            pltpu.VMEM((zs, width, scen), f32),
            pltpu.VMEM((zs, width, scen), f32),
            pltpu.VMEM((width, scen), f32),
            pltpu.VMEM((width, scen), f32),
            pltpu.VMEM((width, scen), f32),
            pltpu.VMEM((node_map.shape[0], scen, scen), f32),
            pltpu.VMEM((8, scen), f32),
            pltpu.VMEM((n, 8, scen), f32),
            dma((zs,)),
            dma((zs,)), dma((zs,)), dma((zs,)), dma((zs,)), dma((2 * zs,)), dma((2 * zs,)),
            dma((2 * zs,)), dma((2 * zs,)), dma((zs,)), dma((zs,)), dma((zs,)), dma((zs,)),
            dma((n,)), dma((n,)),
        ],
        compiler_params=pltpu.CompilerParams(collective_id=0, has_side_effects=True, vmem_limit_bytes=56 << 20),
    )(matrix, bounds_rhs, costs, upper[None, :], bound_mask[None, :], node_map, weights[None, :])
    return pl.pallas_call(
        finish,
        out_shape=(
            jax.ShapeDtypeStruct((width, scen), f32),
            jax.ShapeDtypeStruct((rows, scen), f32),
            jax.ShapeDtypeStruct((width, scen), f32),
            jax.ShapeDtypeStruct((OUTER,), f32),
        ),
        in_specs=[vmem] * 4,
        out_specs=(vmem, vmem, vmem, pl.BlockSpec(memory_space=pltpu.SMEM)),
    )(primal, dual, multipliers, gaps)


def solution(mesh):
    placed = (
        P(("grp", "con"), None),
        P(("grp", "con"), None),
        P(("grp", "con"), None),
        P(("grp", "con")),
        P(("grp", "con")),
        P(None, "grp"),
        P("grp"),
    )
    return jax.shard_map(
        functools.partial(body, mesh.shape["con"]),
        mesh=mesh,
        in_specs=placed,
        out_specs=(
            P(("grp", "con"), None),
            P(("grp", "con"), None),
            P(("grp", "con"), None),
            P("grp"),
        ),
        check_vma=False,
    )
```
